32 devices in a mesh: wide: 4 (over z), narrow: 8 (over y, x, core).
Axes of the slice: x: 2, y: 2, z: 4, core: 2. Of those that a mesh axis runs over, the one named last changes fastest.
Arguments:
- saved_inputs: bfloat16 [1024, 5120], P('wide', 'narrow'), may hold values from -6 to 6
- out_grads: bfloat16 [1024, 5120], P('wide', 'narrow'), may hold values from -48 to 48
- seq_ids: int32 [1024], P('wide'), may hold values from 0 to 7, as said below
- seq_counts: int32 [8], P('wide'), may hold values from 64 to 192, as said below
- basis_in: bfloat16 [5120, 5120], P('narrow'), may hold values from -0.078125 to 0.078125
- basis_out: bfloat16 [5120, 5120], P('narrow'), may hold values from -0.078125 to 0.078125
- query_rotated: bfloat16 [5120, 5120], P('narrow', 'wide'), may hold values from -6 to 6
- damping: float32 [], replicated, may hold values from 0.05 to 0.5
Outputs:
- eigenvalues: float32 [5120, 5120], P('narrow', 'wide')
- preconditioned: float32 [5120, 5120], P('narrow', 'wide')
The draws below stay inside these ranges and needn't reach their ends.
Inputs may be any that keep to these rules, and one draw needn't show every extreme that they name: seq_ids names for each token its sequence; the 256 tokens of block w of the token axis belong to the sequences 2 * w to 2 * w + 1, each having at least one token. seq_counts[s] is the number of tokens whose seq_ids equal s.
All inputs are finite; a program needn't handle non-finite values.
Results may differ from the reference program's by a relative error of at most 0.01.
Values may be sent and summed in bfloat16 or wider, within the bound.
No kernel may reach another device: no remote copies, remote signals or barrier semaphores. Data moves between devices by JAX's collectives and lax.ppermute only.
A program may use at most 128 MiB of HBM per device.

```python
import math
import jax
import jax.numpy as jnp
from jax import lax

D = 5120
TOK_DEV = 256
SEQ_DEV = 2
MAXLEN = 192
TOKENS = 1024
SEQS = 8


def first_lengths(key):
    groups = SEQS // SEQ_DEV
    len_key, pick_key = jax.random.split(jax.random.fold_in(key, 7))
    first_len = jax.random.randint(len_key, (groups,), TOK_DEV - MAXLEN, MAXLEN + 1)
    chosen = jax.random.randint(pick_key, (), 0, groups)
    return jnp.where(jnp.arange(groups) == chosen, MAXLEN, first_len).astype(jnp.int32)


def draw_seq_counts(key, part):
    first_len = first_lengths(key)
    return jnp.stack([first_len, TOK_DEV - first_len], axis=1).reshape(-1).astype(jnp.int32)


def draw_seq_ids(key, part):
    first_len = first_lengths(key)
    groups = first_len.shape[0]
    position = jnp.arange(TOK_DEV, dtype=jnp.int32)[None, :]
    within = jnp.where(position < first_len[:, None], 0, 1).astype(jnp.int32)
    return (within + SEQ_DEV * jnp.arange(groups, dtype=jnp.int32)[:, None]).reshape(-1).astype(jnp.int32)


def block_levels(own_key, shape, shards, smallest, largest):
    factor_of, own = 1.0, jax.random.fold_in(own_key, 6)
    for axis_at, blocks in shards:
        steps = jnp.exp(jax.random.uniform(jax.random.fold_in(own, axis_at), (blocks,), jnp.float32, smallest / len(shards), largest / len(shards)))
        factor_of = factor_of * jnp.repeat(steps, shape[axis_at] // blocks).reshape([-1 if axis == axis_at else 1 for axis in range(len(shape))])
    return factor_of


def gaussian(own_key, shape, scale, limit, pieces=(), held_as=jnp.bfloat16):
    array = jax.random.normal(own_key, shape, jnp.float32) * scale
    if len(pieces) > 0:
        array = block_levels(own_key, shape, pieces, -0.22, 0.18) * array
    return jnp.clip(array, min=-limit, max=limit).astype(held_as)


def setup_inputs(seed: int = 0) -> dict:
    streams_of = jax.random.split(jax.random.key(seed), 9)
    return {
        "saved_inputs": gaussian(streams_of[0], (TOKENS, D), 1.0, 6.0, ((0, 4), (1, 8))),
        "out_grads": gaussian(streams_of[1], (TOKENS, D), 8.0, 48.0, ((0, 4), (1, 8))),
        "seq_ids": draw_seq_ids(jax.random.fold_in(streams_of[8], 71), 0),
        "seq_counts": draw_seq_counts(jax.random.fold_in(streams_of[8], 71), 0),
        "basis_in": gaussian(streams_of[4], (D, D), D ** -0.5, 0.078125, ((0, 8),)),
        "basis_out": gaussian(streams_of[5], (D, D), D ** -0.5, 0.078125, ((0, 8),)),
        "query_rotated": gaussian(streams_of[6], (D, D), 1.0, 6.0, ((0, 8), (1, 4))),
        "damping": jnp.clip(jnp.exp(jax.random.uniform(streams_of[7], (), jnp.float32, math.log(0.05), math.log(0.5))), 0.05, 0.5),
    }


def reference(saved_inputs, out_grads, seq_ids, seq_counts, basis_in, basis_out, query_rotated, damping):
    rot_in = jnp.dot(saved_inputs, basis_in, preferred_element_type=jnp.float32).astype(jnp.bfloat16)
    rot_grad = jnp.dot(out_grads, basis_out, preferred_element_type=jnp.float32).astype(jnp.bfloat16)

    def add_sequence(seq_index, running):
        seq_index = seq_index.astype(jnp.int32)
        group_start = (seq_index // SEQ_DEV) * TOK_DEV
        rows_in = lax.dynamic_slice_in_dim(rot_in, group_start, TOK_DEV, 0)
        rows_grad = lax.dynamic_slice_in_dim(rot_grad, group_start, TOK_DEV, 0)
        seq_here = lax.dynamic_slice_in_dim(seq_ids, group_start, TOK_DEV, 0)
        count = lax.dynamic_slice_in_dim(seq_counts, seq_index, 1, 0)[0].astype(jnp.float32)
        weight = jnp.where(seq_here == seq_index, 1.0, 0.0).astype(jnp.float32) / count
        weighted = (rows_grad.astype(jnp.float32) * weight[:, None]).astype(jnp.bfloat16)
        per_seq = lax.dot_general(weighted, rows_in, (((0,), (0,)), ((), ())), preferred_element_type=jnp.float32)
        return running + per_seq * per_seq

    empty = jnp.zeros((D, D), jnp.float32)
    eigenvalues = lax.fori_loop(0, SEQS, add_sequence, empty) / SEQS
    scaled = (query_rotated.astype(jnp.float32) / (eigenvalues + damping)).astype(jnp.bfloat16)
    middle = jnp.dot(basis_out, scaled, preferred_element_type=jnp.float32).astype(jnp.bfloat16)
    preconditioned = lax.dot_general(middle, basis_in, (((1,), (1,)), ((), ())), preferred_element_type=jnp.float32)
    return eigenvalues, preconditioned
```

```python
import jax
import jax.numpy as jnp
from jax import lax
from jax.sharding import PartitionSpec as P


F32 = jnp.float32
BF16 = jnp.bfloat16


def dot(a, b):
    return jnp.dot(a, b, preferred_element_type=F32)


def build(W, N):
    C = N // 2
    bits = []
    while (2 << len(bits)) < N:
        bits.append(2 << len(bits))
    assert N == 2 * W and (1 << len(bits)) == C

    def swap(x, mask):
        return lax.ppermute(x, "narrow", [(i, i ^ mask) for i in range(N)])

    def ring(x, s=1):
        return lax.ppermute(x, "wide", [(i, (i + s) % W) for i in range(W)])

    def hop(x, frm, to):
        return lax.ppermute(
            x,
            ("wide", "narrow"),
            [
                (z * N + 2 * (z ^ frm) + k, z * N + 2 * (z ^ to) + k)
                for z in range(W)
                for k in range(2)
            ],
        )

    def path(turn):
        nb = len(bits)
        seq = []
        for i in range(C):
            g = i ^ (i >> 1)
            seq.append(sum(((g >> b) & 1) << ((b + turn) % nb) for b in range(nb)))
        return seq

    def reduce_pieces(pieces):
        odd = swap(jnp.stack([pieces[2 * m + 1].astype(BF16) for m in range(C)]), 1)
        even = [(pieces[2 * m] + odd[m].astype(F32)) for m in range(C)]
        total = even[0]
        for m in range(1, C):
            total = total + swap(even[m].astype(BF16), 2 * m).astype(F32)
        return total

    def shards(
        saved_inputs, out_grads, seq_ids, seq_counts, basis_in, basis_out, query_rotated, damping
    ):
        n = lax.axis_index("narrow")
        z = lax.axis_index("wide")
        tok = seq_ids.shape[0]
        seqs = seq_counts.shape[0]
        rows = basis_out.shape[0]
        width = query_rotated.shape[1]
        chunk = 256 if width % 256 == 0 else 128
        J = width // chunk

        xs = [saved_inputs]
        ids = [seq_ids]
        for s in range(1, W):
            xs.append(ring(xs[-1]))
            ids.append(ring(seq_ids, s))

        pieces = [
            dot(out_grads, lax.dynamic_slice_in_dim(basis_out, (n ^ r) * rows, rows, 1))
            for r in range(N)
        ]
        rot_grad = reduce_pieces(pieces).astype(BF16)
        own = seq_ids - z * seqs
        member = own[:, None] == jnp.arange(seqs, dtype=jnp.int32)[None, :]
        weight = jnp.sum(
            jnp.where(member, 1.0, 0.0).astype(F32) / seq_counts.astype(F32)[None, :], axis=1
        )
        wg = [(rot_grad.astype(F32) * weight[:, None]).astype(BF16)]
        for s in range(1, W):
            wg.append(ring(wg[-1]))

        v_cols = lax.dynamic_slice_in_dim(basis_in, z * width, width, 1)
        half = W // 2
        rin = []
        for g in range(2):
            xg = jnp.concatenate(xs[g * half : (g + 1) * half], axis=0)
            part = xg.shape[0] // N
            pg = dot(xg, v_cols)
            mine = reduce_pieces(
                [lax.dynamic_slice_in_dim(pg, (n ^ r) * part, part, 0) for r in range(N)]
            ).astype(BF16)
            got = {0: mine}
            for m in range(1, C):
                got[2 * m] = swap(mine, 2 * m)
            for m in range(C):
                got[2 * m + 1] = swap(got[2 * m], 1)
            order = n ^ jnp.arange(N)
            stacked = jnp.stack([got[r] for r in range(N)])
            rin.append(jnp.take(stacked, order, axis=0).reshape(half, tok, width))
        rin = jnp.concatenate(rin, axis=0)

        masks = []
        for s in range(W):
            local = ids[s] - ((z - s) % W) * seqs
            masks.append(local[None, :] == jnp.arange(seqs, dtype=jnp.int32)[:, None])
        masks = jnp.stack(masks)
        wgs = jnp.stack(wg)
        masked = jnp.where(masks[:, :, :, None], wgs[:, None], jnp.zeros((), BF16))
        per_seq = jnp.einsum("gsti,gtj->gsij", masked, rin, preferred_element_type=F32)
        eigenvalues = jnp.sum(per_seq * per_seq, axis=(0, 1)) / (seqs * W)
        scaled = (query_rotated.astype(F32) / (eigenvalues + damping)).astype(BF16)

        v_own = [
            jnp.concatenate(
                [
                    lax.dynamic_slice_in_dim(
                        basis_in, ((z - s) % W) * width + j * chunk, chunk, 1
                    )
                    for s in range(W)
                ],
                axis=1,
            )
            for j in range(J)
        ]
        role = (n >> 1) ^ z
        v_rows = []
        for j in range(J):
            seq = path(j)
            cur, total = v_own[j], None
            for h in range(C - 1):
                cur = hop(cur, seq[h], seq[h + 1])
                total = cur if total is None else total + cur
            mine = jnp.where(role == 0, v_own[j], total)
            other = swap(mine, 1)
            low = (n & 1) == 0
            v_rows.append(
                jnp.concatenate([jnp.where(low, mine, other), jnp.where(low, other, mine)], axis=0)
            )

        vo = jnp.concatenate(
            [lax.dynamic_slice_in_dim(basis_out, (n ^ r) * rows, rows, 1) for r in range(N)], axis=1
        )
        out = None
        for j in range(J):
            got = {0: scaled[:, j * chunk : (j + 1) * chunk]}
            turn = j % len(bits)
            for b in bits[turn:] + bits[:turn]:
                for m in list(got):
                    got[m ^ b] = swap(got[m], b)
            for m in list(got):
                got[m ^ 1] = swap(got[m], 1)
            s_all = jnp.concatenate([got[r] for r in range(N)], axis=0)
            us = [dot(vo, s_all).astype(BF16)]
            for s in range(1, W):
                us.append(ring(us[-1]))
            part = lax.dot_general(
                jnp.concatenate(us, axis=1),
                v_rows[j],
                (((1,), (1,)), ((), ())),
                preferred_element_type=F32,
            )
            out = part if out is None else out + part
        return (eigenvalues, out)

    return shards


def solution(mesh):
    return jax.shard_map(
        build(mesh.shape["wide"], mesh.shape["narrow"]),
        mesh=mesh,
        in_specs=(
            P("wide", "narrow"),
            P("wide", "narrow"),
            P("wide"),
            P("wide"),
            P("narrow", None),
            P("narrow", None),
            P("narrow", "wide"),
            P(),
        ),
        out_specs=(P("narrow", "wide"), P("narrow", "wide")),
        check_vma=False,
    )
```
